32 devices in a mesh: rep: 2 (over y), seq: 4 (over z), ch: 4 (over x, core).
Axes of the slice: x: 2, y: 2, z: 4, core: 2. Of those that a mesh axis runs over, the one named last changes fastest.
Arguments:
- key_proj: bfloat16 [4096, 4096], P(('rep', 'seq'), 'ch'), parts along dimension 0, may hold values from -6 to 6
- value_proj: bfloat16 [4096, 4096], P(('rep', 'seq'), 'ch'), parts along dimension 0, may hold values from -6 to 6
- query_proj: bfloat16 [4096, 4096], P(('rep', 'seq'), 'ch'), parts along dimension 0, may hold values from -6 to 6
- filters: bfloat16 [256, 2048], P('ch', 'seq'), may hold values from -3 to 3
- sources: int32 [8], P('rep'), parts along dimension 0, may hold values from 0 to 15, as said below
- owner: int32 [32], P('rep'), parts along dimension 0, may hold values from 0 to 3, as said below
Outputs:
- conv_out: bfloat16 [4096, 4096], P(('rep', 'seq'), 'ch'), parts along dimension 0
The draws below stay inside these ranges and needn't reach their ends.
There are 2 independent parts, one for each index of `rep`. The reference program is written for one: setup_inputs(seed, part) draws one part's arguments, and reference() takes and returns one part's arrays. A program takes and returns all parts, laid end to end along the dimension named above; an argument that names none is the same for every part. Nothing has to cross between parts.
Inputs may be any that keep to these rules, and one draw needn't show every extreme that they name: `sources`: four distinct stretch numbers in increasing order; the first is 0 and the last 15. owner[k] is the index along seq of the shard holding stretch k; every shard holds exactly 4 stretches, stored one after another in increasing stretch number.
All inputs are finite; a program needn't handle non-finite values.
Results may differ from the reference program's by a relative error of at most 0.0049.
Values may be sent and summed in bfloat16 or wider, within the bound.
A program may use at most 64 MiB of HBM per device.

```python
import math
import jax
import jax.numpy as jnp
from jax import lax

D = 4096
GROUP_CH = 16
FILTER_GROUPS = 256
STRETCH = 128
WIN = 4
CH_DEV = 4
NCH = 16
SEQUENCE_LENGTH = 2048


def channel_offsets(key):
    sign_key, size_key = jax.random.split(jax.random.fold_in(key, 31))
    signs = jnp.where(jax.random.uniform(sign_key, (D,)) < 0.5, -1.0, 1.0)
    return signs * jax.random.uniform(size_key, (D,), minval=0.7, maxval=1.3)


def stretch_levels(key, salt):
    level_key = jax.random.fold_in(key, salt)
    return jnp.exp(jax.random.uniform(level_key, (NCH, 1, 1), minval=-4.0, maxval=1.0))


def draw_key_proj(key, part):
    offsets = channel_offsets(key)
    levels = stretch_levels(key, 41)
    noise_key = jax.random.fold_in(key, 43)
    noise = jax.random.normal(noise_key, (NCH, STRETCH, D))
    rows = jnp.clip(levels * (noise + offsets[None, None, :]), -6.0, 6.0)
    return rows.reshape(SEQUENCE_LENGTH, D).astype(jnp.bfloat16)


def draw_value_proj(key, part):
    offsets = channel_offsets(key)
    levels = stretch_levels(key, 47)
    noise_key = jax.random.fold_in(key, 53)
    noise = jax.random.normal(noise_key, (NCH, STRETCH, D))
    rows = jnp.clip(levels * (noise + offsets[None, None, :]), -6.0, 6.0)
    return rows.reshape(SEQUENCE_LENGTH, D).astype(jnp.bfloat16)


def draw_filters(key, part):
    first, second, third, fourth_random_key, fifth = jax.random.split(jax.random.fold_in(key, 7), 5)
    lag_dimension = jnp.arange(SEQUENCE_LENGTH, dtype=jnp.float32)
    quick = float(min(40, max(4, STRETCH // 2)))
    slow_share = 0.5
    slow_flag = jax.random.uniform(first, (FILTER_GROUPS, 1)) < slow_share
    fast_log = jax.random.uniform(second, (FILTER_GROUPS, 1), minval=math.log(quick), maxval=math.log(float(SEQUENCE_LENGTH)))
    slow_log = jax.random.uniform(third, (FILTER_GROUPS, 1), minval=math.log(float(SEQUENCE_LENGTH)), maxval=math.log(50.0 * SEQUENCE_LENGTH))
    decay_len = jnp.exp(jnp.where(slow_flag, slow_log, fast_log))
    spike_lag_offset = jax.random.randint(fourth_random_key, (FILTER_GROUPS, 3, 1), 1, SEQUENCE_LENGTH).astype(jnp.float32)
    retained_fraction = jax.random.uniform(fifth, (FILTER_GROUPS, 3, 1), minval=0.5, maxval=0.8)
    discarded_mask = jnp.prod(jnp.where(lag_dimension[None, None, :] >= spike_lag_offset, retained_fraction, 1.0), axis=1)
    scale = 1.0 / jnp.sqrt(jnp.minimum(decay_len, float(STRETCH)))
    noise_key = jax.random.fold_in(key, 13)
    rough = jnp.clip(jax.random.normal(noise_key, (FILTER_GROUPS, SEQUENCE_LENGTH)), -6.0, 6.0)
    near_part = rough * jnp.exp(-lag_dimension[None, :] / decay_len) * discarded_mask * scale
    sign_key = jax.random.fold_in(key, 17)
    tail_sign = jnp.where(jax.random.uniform(sign_key, (FILTER_GROUPS, 1)) < 0.5, -1.0, 1.0)
    tail_rough = 0.25 + 1.5 * jax.random.uniform(jax.random.fold_in(key, 19), (FILTER_GROUPS, SEQUENCE_LENGTH))
    tail_part = 0.015 * scale * tail_sign * tail_rough * jnp.exp(-lag_dimension[None, :] / (2.0 * SEQUENCE_LENGTH))
    return (near_part + tail_part).astype(jnp.bfloat16)


def draw_sources(key, part):
    inner = jax.random.permutation(jax.random.fold_in(key, 11), NCH - 2)[:2] + 1
    lower = jnp.minimum(inner[0], inner[1])
    upper = jnp.maximum(inner[0], inner[1])
    return jnp.stack([jnp.int32(0), lower.astype(jnp.int32), upper.astype(jnp.int32), jnp.int32(NCH - 1)]).astype(jnp.int32)


def draw_owner(key, part):
    shuffled = jax.random.permutation(jax.random.fold_in(key, 23), NCH)
    return (shuffled // CH_DEV).astype(jnp.int32)


def level_of(rng, dims, shards, smallest, largest):
    def one(dim, parts):
        draws = jax.random.uniform(jax.random.fold_in(jax.random.fold_in(rng, 6), dim), (parts,), jnp.float32, smallest / len(shards), largest / len(shards))
        return jnp.repeat(jnp.exp(draws), dims[dim] // parts).reshape((-1,) + (1,) * (len(dims) - dim - 1))

    factor_of = one(*shards[0])
    for cut in shards[1:]:
        factor_of = factor_of * one(*cut)
    return factor_of


def bell_draw(stream_key, extent, deviation, bound, shards=(), kind=jnp.bfloat16):
    array = deviation * jax.random.normal(stream_key, extent, jnp.float32)
    if shards:
        array = array * level_of(stream_key, extent, shards, -0.22, 0.18)
    return jnp.clip(array, -bound, bound).astype(kind)


def setup_inputs(seed: int = 0, part: int = 0) -> dict:
    seeds = jax.random.split(jax.random.key(seed), 7)
    part_keys = jax.random.split(jax.random.fold_in(seeds[6], part), 7)
    return {
        "key_proj": draw_key_proj(jax.random.fold_in(jax.random.fold_in(seeds[6], part), 71), part),
        "value_proj": draw_value_proj(jax.random.fold_in(jax.random.fold_in(seeds[6], part), 71), part),
        "query_proj": bell_draw(part_keys[2], (SEQUENCE_LENGTH, D), 1.0, 6.0, ((0, 4), (1, 4))),
        "filters": draw_filters(jax.random.fold_in(seeds[6], 71), part),
        "sources": draw_sources(jax.random.fold_in(jax.random.fold_in(seeds[6], part), 71), part),
        "owner": draw_owner(jax.random.fold_in(jax.random.fold_in(seeds[6], part), 71), part),
    }


def reference(key_proj, value_proj, query_proj, filters, sources, owner):
    stretch_total = owner.shape[0]
    channels = key_proj.shape[1]
    group_count = channels // GROUP_CH
    numbers = jnp.arange(stretch_total, dtype=jnp.int32)
    same_owner = (owner[:, None] == owner[None, :]).astype(jnp.int32)
    earlier = (numbers[None, :] < numbers[:, None]).astype(jnp.int32)
    position = (owner * CH_DEV + jnp.sum(same_owner * earlier, axis=1)).astype(jnp.int32)
    stretch_at = jnp.sum((position[None, :] == numbers[:, None]).astype(jnp.int32) * numbers[None, :], axis=1).astype(jnp.int32)
    source_at = jnp.sum((sources[:, None] == numbers[None, :]).astype(jnp.int32) * position[None, :], axis=1).astype(jnp.int32)
    gated = (key_proj.astype(jnp.float32) * value_proj.astype(jnp.float32)).astype(jnp.bfloat16)
    blocks = gated.reshape(stretch_total, STRETCH, group_count, GROUP_CH)
    window = jnp.take(blocks, source_at, axis=0).astype(jnp.float32)
    padded = jnp.concatenate([jnp.zeros((group_count, STRETCH), jnp.float32), filters.astype(jnp.float32)], axis=1)
    offsets = (STRETCH + jnp.arange(STRETCH, dtype=jnp.int32)[:, None] - jnp.arange(STRETCH, dtype=jnp.int32)[None, :]).astype(jnp.int32)

    def one_block(stored):
        target = stretch_at[stored]
        summed = jnp.zeros((STRETCH, group_count, GROUP_CH), jnp.float32)
        for window_slot in range(WIN):
            lag_block = target - sources[window_slot]
            lag_start = (jnp.maximum(lag_block, 0) * STRETCH).astype(jnp.int32)
            lag_span = lax.dynamic_slice_in_dim(padded, lag_start, 2 * STRETCH, 1)
            toeplitz = jnp.take(lag_span, offsets, axis=1)
            term = jnp.einsum("gij,jgc->igc", toeplitz, window[window_slot], precision=lax.Precision.HIGHEST)
            summed = summed + jnp.where(lag_block >= 0, term, 0.0)
        gate_rows = lax.dynamic_slice_in_dim(query_proj, (stored * STRETCH).astype(jnp.int32), STRETCH, 0).astype(jnp.float32)
        return (gate_rows * summed.reshape(STRETCH, channels)).astype(jnp.bfloat16)

    result = lax.map(one_block, numbers)
    return result.reshape(stretch_total * STRETCH, channels)
```

```python
import functools

import jax
import jax.numpy as jnp
from jax import lax
from jax.experimental import pallas as pl
from jax.experimental.pallas import tpu as pltpu
from jax.sharding import PartitionSpec as P

STRETCH = 128
WIN = 4
SENT = WIN - 1
PIECE = 16
OCT = 8
QUAD = 4
SPLIT = 2
HOP = 6
F32 = jnp.float32
BF16 = jnp.bfloat16
CONV = F32


def swap_halves(low, high):
    keep = lax.broadcasted_iota(jnp.int32, low.shape, 1) < 64
    return (
        jnp.where(keep, low, pltpu.roll(high, 64, 1)),
        jnp.where(keep, pltpu.roll(low, 64, 1), high),
    )


def shifted(pieces):
    keep = lax.broadcasted_iota(jnp.int32, pieces[0].shape, 1) < 64
    zero = jnp.zeros_like(pieces[0])
    turned = [pltpu.roll(piece, 64, 1) for piece in pieces]
    blocks = [jnp.where(keep, zero, piece) for piece in turned]
    blocks += pieces
    blocks += [jnp.where(keep, piece, zero) for piece in turned]
    return blocks


def turn_filters(shards_ref, padded_ref):
    count, halves, groups, span = shards_ref.shape
    width = padded_ref.shape[1]
    lags = count * span
    row = lax.broadcasted_iota(jnp.int32, (128, 128), 0)
    col = lax.broadcasted_iota(jnp.int32, (128, 128), 1)
    flip = (row + col == 127).astype(BF16)
    for n in range(lags // 128):
        at = lags - 128 * (n + 1)
        lanes = slice(at % span, at % span + 128)
        chunk = jnp.concatenate([shards_ref[at // span, h, :, lanes] for h in range(halves)], axis=0)
        padded_ref[:, 128 * n : 128 * (n + 1)] = jnp.dot(chunk, flip, preferred_element_type=F32)
    padded_ref[:, lags:] = jnp.zeros((halves * groups, width - lags), F32)


def fused_kernel(
    size, halves, sources_hbm, owner_hbm, key_hbm, value_hbm, query_hbm, filters_hbm,
    out_ref, sources_ref, owner_ref, key_first, value_first, key_ref, value_ref, query_ref,
    both_ref, own_ref, from_left_ref, from_right_ref, taps_ref, padded_ref, g_even_ref, g_odd_ref,
    conv_ref,
    scalar_sem, own_sem, key_sem, value_sem, query_sem,
    tap_right_send, tap_left_send, tap_recv, tap_across_send, tap_across_recv,
    right_send, right_recv, left_send, left_recv,
):
    stretches = owner_ref.shape[0]
    slots = key_ref.shape[1]
    octets = out_ref.shape[1] // 128
    width = padded_ref.shape[1]
    last = stretches - 1
    per_quad = QUAD // SPLIT
    per_octet = 2 * per_quad
    chunks = octets * per_octet
    me = lax.axis_index("seq")
    half = lax.axis_index("rep") if halves == 2 else 0
    has_left = me > 0
    has_right = me < size - 1

    def remote(src, dst, send, recv, device):
        return pltpu.make_async_remote_copy(
            src_ref=src, dst_ref=dst, send_sem=send, recv_sem=recv,
            device_id=device, device_id_type=pl.DeviceIdType.MESH,
        )

    def tap_hop(shard, step):
        send = tap_right_send if step > 0 else tap_left_send
        part = taps_ref.at[shard, half]
        return remote(part, part, send.at[shard], tap_recv.at[shard], {"seq": me + step})

    def tap_across(shard, part):
        block = taps_ref.at[shard, part]
        return remote(
            block, block, tap_across_send.at[shard], tap_across_recv.at[shard], {"rep": 1 - half}
        )

    def right_hop(c):
        return remote(
            both_ref.at[0, c], from_left_ref.at[c], right_send.at[c], right_recv.at[c],
            {"seq": me + 1},
        )

    def left_hop(c):
        return remote(
            both_ref.at[1, c], from_right_ref.at[c], left_send.at[c], left_recv.at[c],
            {"seq": me - 1},
        )

    def lanes_of(o):
        if isinstance(o, int):
            return pl.ds(128 * o, 128)
        return pl.ds(pl.multiple_of(o * 128, 128), 128)

    def load(src, dst, sem, o):
        return pltpu.make_async_copy(src.at[:, :, lanes_of(o)], dst, sem.at[o])

    scalars = [
        pltpu.make_async_copy(src, dst, scalar_sem.at[i])
        for i, (src, dst) in enumerate(((sources_hbm, sources_ref), (owner_hbm, owner_ref)))
    ]
    for scalar in scalars:
        scalar.start()
    own_taps = pltpu.make_async_copy(filters_hbm, taps_ref.at[me], own_sem)
    own_taps.start()
    load(key_hbm, key_first, key_sem, 0).start()
    load(value_hbm, value_first, value_sem, 0).start()

    barrier = pltpu.get_barrier_semaphore()

    for step, there in ((-1, has_left), (1, has_right)):
        @pl.when(there)
        def _():
            pl.semaphore_signal(
                barrier, inc=1, device_id={"seq": me + step}, device_id_type=pl.DeviceIdType.MESH
            )

    if halves == 2:
        pl.semaphore_signal(
            barrier, inc=1, device_id={"rep": 1 - half}, device_id_type=pl.DeviceIdType.MESH
        )

    @pl.loop(1, octets)
    def _(o):
        load(key_hbm, key_ref.at[o - 1], key_sem, o).start()
        load(value_hbm, value_ref.at[o - 1], value_sem, o).start()

    query_load = pltpu.make_async_copy(query_hbm, query_ref, query_sem)
    query_load.start()

    own_taps.wait()
    others = has_left.astype(jnp.int32) + has_right.astype(jnp.int32)
    pl.semaphore_wait(barrier, others + (1 if halves == 2 else 0))
    for step, there in ((-1, has_left), (1, has_right)):
        @pl.when(there)
        def _():
            tap_hop(me, step).start()

    for scalar in scalars:
        scalar.wait()
    source = [sources_ref[w] for w in range(WIN)]
    source_owner = [jnp.int32(0)] * WIN
    source_slot = [jnp.int32(0)] * WIN
    slot_stretch = [jnp.int32(0)] * slots
    source_owner = [owner_ref[source[w]] for w in range(WIN)]
    count = jnp.int32(0)
    for k in range(stretches):
        holder = owner_ref[k]
        for w in range(WIN - 1):
            source_slot[w] += jnp.where((holder == source_owner[w]) & (k < source[w]), 1, 0)
        here = holder == me
        for t in range(slots):
            slot_stretch[t] += jnp.where(here & (count == t), k, 0)
        count += jnp.where(here, 1, 0)
    first = [
        [last - jnp.maximum(slot_stretch[t] - source[w], -1) for w in range(WIN)]
        for t in range(slots)
    ]
    way = [jnp.where(source_owner[w] <= me, 0, 1) for w in range(WIN - 1)]

    def splat(value):
        return jnp.full((PIECE, 128), value, jnp.int32)

    mine = [splat(source_owner[w]) == me for w in range(WIN)]

    def prepare(o, keys, values):
        for w in range(WIN):
            slot = source_slot[w] if w < SENT else slots - 1
            parts = []
            for e in range(OCT):
                rows = pl.ds(PIECE * e, PIECE)
                parts.append(
                    (keys[slot, rows, :].astype(F32) * values[slot, rows, :].astype(F32)).astype(BF16)
                )
            for p in range(QUAD):
                for quad, part in enumerate(swap_halves(parts[p], parts[p + QUAD])):
                    c, at = o * per_octet + quad * per_quad + p // SPLIT, p % SPLIT
                    if w < SENT:
                        both_ref[0, c, w, at] = part
                        both_ref[1, c, w, at] = part
                    else:
                        own_ref[c, at] = jnp.where(mine[w], part, jnp.zeros_like(part))

    def merge(way, c, arrived):
        for w in range(SENT):
            for at in range(SPLIT):
                both_ref[way, c, w, at] = jnp.where(
                    mine[w], both_ref[way, c, w, at], arrived[c, w, at]
                )

    load(key_hbm, key_first, key_sem, 0).wait()
    load(value_hbm, value_first, value_sem, 0).wait()
    prepare(0, key_first, value_first)

    @pl.loop(1, octets)
    def _(o):
        load(key_hbm, key_ref.at[o - 1], key_sem, o).wait()
        load(value_hbm, value_ref.at[o - 1], value_sem, o).wait()

    right_lag = HOP * me
    left_lag = HOP * (size - 1 - me)
    lag = jnp.maximum(right_lag, left_lag)
    drain = HOP * (size - 1)

    def spread(quad, g_ref):
        for g in range(QUAD):
            row = jnp.broadcast_to(padded_ref[pl.ds(quad * QUAD + g, 1), :], (PIECE, width))
            turned = pltpu.roll(row, width - 15, 1, stride=1, stride_axis=0).astype(BF16)
            for n in range(stretches + 2):
                g_ref[g, n] = turned[:, 128 * n : 128 * (n + 1)]

    def compute(quad, which):
        g_ref, next_ref = ((g_even_ref, g_odd_ref), (g_odd_ref, g_even_ref))[which]
        spread(jnp.minimum(quad + 1, 2 * octets - 1), next_ref)
        blocks = []
        for w in range(WIN):
            pieces = []
            for p in range(QUAD):
                c, at = quad * per_quad + p // SPLIT, p % SPLIT
                pieces.append(both_ref[way[w], c, w, at] if w < SENT else own_ref[c, at])
            blocks.append(shifted(pieces))
        zero = jnp.zeros_like(blocks[0][0])

        def column(turn):
            return jnp.concatenate(
                [
                    blocks[w][turn + n - 3] if 0 <= turn + n - 3 < 3 * QUAD else zero
                    for w in range(WIN)
                    for n in range(2 * OCT)
                ],
                axis=0,
            )

        taps = jnp.concatenate(
            [
                jnp.concatenate(
                    [g_ref[g, first[t][w] + h] for w in range(WIN) for h in range(2)], axis=1
                )
                for g in range(QUAD)
                for t in range(slots)
            ],
            axis=0,
        )
        group = lax.broadcasted_iota(jnp.int32, (slots * PIECE, 128), 1) // PIECE % QUAD
        for pair in range(2):
            columns = jnp.concatenate([column(2 * pair), column(2 * pair + 1)], axis=1)
            conv = jnp.dot(taps, columns, preferred_element_type=F32)
            for turn in range(2):
                lanes = slice(128 * turn, 128 * (turn + 1))
                rows = [
                    conv[slots * PIECE * g : slots * PIECE * (g + 1), lanes] for g in range(QUAD)
                ]
                conv_ref[which, 2 * pair + turn] = jnp.where(
                    group < 2,
                    jnp.where(group < 1, rows[0], rows[1]),
                    jnp.where(group < 3, rows[2], rows[3]),
                ).astype(CONV)

    def finish(o):
        lanes = lanes_of(o)
        for t in range(slots):
            for turn in range(QUAD):
                rows = slice(PIECE * t, PIECE * (t + 1))
                for half, part in enumerate(
                    swap_halves(conv_ref[0, turn, rows, :], conv_ref[1, turn, rows, :])
                ):
                    start = STRETCH * t + STRETCH // 2 * half + PIECE * turn
                    at = (slice(start, start + PIECE), lanes)
                    out_ref[at] = (query_ref[at].astype(F32) * part.astype(F32)).astype(BF16)

    @pl.loop(0, chunks + HOP * (size - 1))
    def _(s):
        far = s // HOP
        for step, onward in ((-1, has_right), (1, has_left)):
            shard = me + step * far
            @pl.when((s % HOP == 0) & (far >= 1) & (shard >= 0) & (shard < size))
            def _():
                tap_hop(shard, -step).wait_recv()

                @pl.when(onward)
                def _():
                    tap_hop(shard, -step).start()

                if halves == 2:
                    tap_across(shard, half).start()

        @pl.when((s >= right_lag) & (s < right_lag + chunks))
        def _():
            c = s - right_lag

            @pl.when(has_left)
            def _():
                right_hop(c).wait_recv()
                merge(0, c, from_left_ref)

            @pl.when(has_right)
            def _():
                right_hop(c).start()

        @pl.when((s >= drain) & has_right)
        def _():
            right_hop(s - drain).wait_send()

        @pl.when((s >= drain) & has_left)
        def _():
            left_hop(s - drain).wait_send()

        @pl.when((s >= left_lag) & (s < left_lag + chunks))
        def _():
            c = s - left_lag

            @pl.when(has_right)
            def _():
                left_hop(c).wait_recv()
                merge(1, c, from_right_ref)

            @pl.when(has_left)
            def _():
                left_hop(c).start()

        @pl.when((s % per_octet == 0) & (s // per_octet + 1 < octets))
        def _():
            o = s // per_octet
            prepare(o + 1, key_ref.at[o], value_ref.at[o])

        @pl.when(s == lag)
        def _():
            if halves == 2:
                for shard in range(size):
                    @pl.when(me != shard)
                    def _():
                        tap_across(shard, 1 - half).wait_recv()
            turn_filters(taps_ref, padded_ref)
            spread(0, g_even_ref)
            query_load.wait()

        for which in range(2):
            @pl.when(
                (s >= lag) & (s < lag + chunks)
                & ((s - lag) % per_octet == per_quad * (which + 1) - 1)
            )
            def _():
                compute((s - lag) // per_quad, which)
                if which == 1:
                    finish((s - lag) // per_octet)

        shard = s - drain

        @pl.when((shard >= 0) & (shard <= me) & has_right)
        def _():
            tap_hop(shard, 1).wait_send()

        @pl.when((shard >= me) & (shard < size) & has_left)
        def _():
            tap_hop(shard, -1).wait_send()

        if halves == 2:
            @pl.when((shard >= 0) & (shard < size) & (shard != me))
            def _():
                tap_across(shard, half).wait_send()


def shards(size, reps, key_proj, value_proj, query_proj, filters, sources, owner):
    rows, channels = key_proj.shape
    groups, span = filters.shape
    stretches = owner.shape[0]
    octets = channels // 128
    slots = rows // STRETCH
    lags = size * span
    chunks = groups // SPLIT
    halves = 2 if reps == 2 else 1
    by_slot = (slots, STRETCH, channels)
    key_proj, value_proj = key_proj.reshape(by_slot), value_proj.reshape(by_slot)
    filters = filters.reshape(halves, groups // halves, span)
    vmem = pl.BlockSpec(memory_space=pltpu.VMEM)
    hbm = pl.BlockSpec(memory_space=pltpu.HBM)
    chunk = (chunks, SENT, SPLIT, PIECE, 128)
    dma = pltpu.SemaphoreType.DMA
    return pl.pallas_call(
        functools.partial(fused_kernel, size, halves),
        out_shape=jax.ShapeDtypeStruct((rows, channels), BF16),
        in_specs=[hbm] * 6,
        out_specs=vmem,
        scratch_shapes=[
            pltpu.SMEM(sources.shape, jnp.int32), pltpu.SMEM(owner.shape, jnp.int32),
            pltpu.VMEM((slots, STRETCH, 128), BF16), pltpu.VMEM((slots, STRETCH, 128), BF16),
            pltpu.VMEM((octets - 1, slots, STRETCH, 128), BF16),
            pltpu.VMEM((octets - 1, slots, STRETCH, 128), BF16),
            pltpu.VMEM((rows, channels), BF16),
            pltpu.VMEM((2,) + chunk, BF16),
            pltpu.VMEM((chunks, SPLIT, PIECE, 128), BF16),
            pltpu.VMEM(chunk, BF16), pltpu.VMEM(chunk, BF16),
            pltpu.VMEM((size, halves, groups // halves, span), BF16),
            pltpu.VMEM((groups, lags + 256), F32),
            pltpu.VMEM((QUAD, stretches + 2, PIECE, 128), BF16),
            pltpu.VMEM((QUAD, stretches + 2, PIECE, 128), BF16),
            pltpu.VMEM((2, QUAD, slots * PIECE, 128), CONV),
            dma((2,)), dma, dma((octets,)), dma((octets,)), dma,
            dma((size,)), dma((size,)), dma((size,)), dma((size,)), dma((size,)),
            dma((chunks,)), dma((chunks,)), dma((chunks,)), dma((chunks,)),
        ],
        compiler_params=pltpu.CompilerParams(
            vmem_limit_bytes=55312384, collective_id=0, has_side_effects=True
        ),
    )(sources, owner, key_proj, value_proj, query_proj, filters)


def solution(mesh):
    return jax.shard_map(
        functools.partial(shards, mesh.shape["seq"], mesh.shape["rep"]),
        mesh=mesh,
        in_specs=(
            P(("rep", "seq"), "ch"),
            P(("rep", "seq"), "ch"),
            P(("rep", "seq"), "ch"),
            P("ch", "seq"),
            P("rep"),
            P("rep"),
        ),
        out_specs=P(("rep", "seq"), "ch"),
        check_vma=False,
    )
```

```python
import functools

import jax
import jax.numpy as jnp
from jax import lax
from jax.experimental import pallas as pl
from jax.experimental.pallas import tpu as pltpu
from jax.sharding import PartitionSpec as P

STRETCH = 128
WIN = 4
SENT = WIN - 1
PIECE = 16
OCT = 8
QUAD = 4
SPLIT = 2
HOP = 6
LEAD = 4
AHEAD = 8
F32 = jnp.float32
BF16 = jnp.bfloat16
CONV = F32


def swap_halves(low, high):
    keep = lax.broadcasted_iota(jnp.int32, low.shape, 1) < 64
    return (
        jnp.where(keep, low, pltpu.roll(high, 64, 1)),
        jnp.where(keep, pltpu.roll(low, 64, 1), high),
    )


def shifted(pieces):
    keep = lax.broadcasted_iota(jnp.int32, pieces[0].shape, 1) < 64
    zero = jnp.zeros_like(pieces[0])
    turned = [pltpu.roll(piece, 64, 1) for piece in pieces]
    blocks = [jnp.where(keep, zero, piece) for piece in turned]
    blocks += pieces
    blocks += [jnp.where(keep, piece, zero) for piece in turned]
    return blocks


def turn_filters(shards_ref, half, padded_ref):
    count, halves, groups, span = shards_ref.shape
    width = padded_ref.shape[1]
    lags = count * span
    row = lax.broadcasted_iota(jnp.int32, (128, 128), 0)
    col = lax.broadcasted_iota(jnp.int32, (128, 128), 1)
    flip = (row + col == 127).astype(BF16)
    rows = pl.ds(pl.multiple_of(half * groups, groups), groups) if halves == 2 else slice(None)
    for n in range(lags // 128):
        at = lags - 128 * (n + 1)
        chunk = shards_ref[at // span, half, :, at % span : at % span + 128]
        padded_ref[rows, 128 * n : 128 * (n + 1)] = jnp.dot(chunk, flip, preferred_element_type=F32)
    padded_ref[rows, lags:] = jnp.zeros((groups, width - lags), F32)


def fused_kernel(
    size, halves, sources_hbm, owner_hbm, key_hbm, value_hbm, query_hbm, filters_hbm,
    out_any, sources_ref, owner_ref, key_first, value_first, key_ref, value_ref, query_ref,
    out_ref, both_ref, own_ref, from_left_ref, from_right_ref, taps_ref, padded_ref, g_even_ref, g_odd_ref,
    conv_ref,
    scalar_sem, own_sem, load_sem, query_sem, store_sem,
    tap_right_send, tap_left_send, tap_recv, tap_across_send, tap_across_recv,
    right_send, right_recv, left_send, left_recv,
):
    stretches = owner_ref.shape[0]
    slots = key_ref.shape[0]
    octets = out_any.shape[1] // 128
    width = padded_ref.shape[1]
    last = stretches - 1
    per_quad = QUAD // SPLIT
    per_octet = 2 * per_quad
    chunks = octets * per_octet
    me = lax.axis_index("seq")
    half = lax.axis_index("rep") if halves == 2 else 0
    part_rows = padded_ref.shape[0] // halves
    has_left = me > 0
    has_right = me < size - 1

    def remote(src, dst, send, recv, device):
        return pltpu.make_async_remote_copy(
            src_ref=src, dst_ref=dst, send_sem=send, recv_sem=recv,
            device_id=device, device_id_type=pl.DeviceIdType.MESH,
        )

    def tap_hop(shard, step):
        send = tap_right_send if step > 0 else tap_left_send
        part = taps_ref.at[shard, half]
        return remote(part, part, send.at[shard], tap_recv.at[shard], {"seq": me + step})

    def tap_across(shard, part):
        block = taps_ref.at[shard, part]
        return remote(
            block, block, tap_across_send.at[shard], tap_across_recv.at[shard], {"rep": 1 - half}
        )

    def right_hop(c):
        return remote(
            both_ref.at[0, c], from_left_ref.at[c], right_send.at[c % AHEAD], right_recv.at[c],
            {"seq": me + 1},
        )

    def left_hop(c):
        return remote(
            both_ref.at[1, c], from_right_ref.at[c], left_send.at[c % AHEAD], left_recv.at[c],
            {"seq": me - 1},
        )

    def lanes_of(o):
        if isinstance(o, int):
            return pl.ds(128 * o, 128)
        return pl.ds(pl.multiple_of(o * 128, 128), 128)

    def place(o):
        return (o + half * (octets // 2)) % octets

    def store(o):
        at = lanes_of(place(o))
        return pltpu.make_async_copy(out_ref.at[:, at], out_any.at[:, at], store_sem.at[o % 2])

    first_lanes = lanes_of(place(0))
    first_loads = [
        pltpu.make_async_copy(src.at[:, :, first_lanes], dst, load_sem.at[i])
        for i, (src, dst) in enumerate(((key_hbm, key_first), (value_hbm, value_first)))
    ]
    loads = [
        pltpu.make_async_copy(src, dst, load_sem.at[2 + i])
        for i, (src, dst) in enumerate(((key_hbm, key_ref), (value_hbm, value_ref)))
    ]

    barrier = pltpu.get_barrier_semaphore()

    for step, there in ((-1, has_left), (1, has_right)):
        @pl.when(there)
        def _():
            pl.semaphore_signal(
                barrier, inc=1, device_id={"seq": me + step}, device_id_type=pl.DeviceIdType.MESH
            )

    if halves == 2:
        pl.semaphore_signal(
            barrier, inc=1, device_id={"rep": 1 - half}, device_id_type=pl.DeviceIdType.MESH
        )

    scalars = [
        pltpu.make_async_copy(src, dst, scalar_sem.at[i])
        for i, (src, dst) in enumerate(((sources_hbm, sources_ref), (owner_hbm, owner_ref)))
    ]
    for scalar in scalars:
        scalar.start()
    own_taps = pltpu.make_async_copy(filters_hbm, taps_ref.at[me], own_sem)
    for copy in first_loads:
        copy.start()
    own_taps.start()
    for copy in loads:
        copy.start()
    query_load = pltpu.make_async_copy(query_hbm, query_ref, query_sem)
    query_load.start()

    for scalar in scalars:
        scalar.wait()
    source = [sources_ref[w] for w in range(WIN)]
    source_owner = [jnp.int32(0)] * WIN
    source_slot = [jnp.int32(0)] * WIN
    slot_stretch = [jnp.int32(0)] * slots
    source_owner = [owner_ref[source[w]] for w in range(WIN)]
    count = jnp.int32(0)
    for k in range(stretches):
        holder = owner_ref[k]
        for w in range(WIN - 1):
            source_slot[w] += jnp.where((holder == source_owner[w]) & (k < source[w]), 1, 0)
        here = holder == me
        for t in range(slots):
            slot_stretch[t] += jnp.where(here & (count == t), k, 0)
        count += jnp.where(here, 1, 0)
    first = [
        [last - jnp.maximum(slot_stretch[t] - source[w], -1) for w in range(WIN)]
        for t in range(slots)
    ]
    way = [jnp.where(source_owner[w] <= me, 0, 1) for w in range(WIN - 1)]

    def splat(value):
        return jnp.full((PIECE, 128), value, jnp.int32)

    mine = [splat(source_owner[w]) == me for w in range(WIN)]

    def prepare(o, at_of, keys, values):
        for w in range(WIN):
            slot = source_slot[w] if w < SENT else slots - 1
            parts = []
            for e in range(OCT):
                at = at_of(slot, pl.ds(PIECE * e, PIECE))
                parts.append((keys[at].astype(F32) * values[at].astype(F32)).astype(BF16))
            for p in range(QUAD):
                for quad, part in enumerate(swap_halves(parts[p], parts[p + QUAD])):
                    c, at = o * per_octet + quad * per_quad + p // SPLIT, p % SPLIT
                    if w < SENT:
                        both_ref[0, c, w, at] = part
                        both_ref[1, c, w, at] = part
                    else:
                        own_ref[c, at] = jnp.where(mine[w], part, jnp.zeros_like(part))

    def merge(way, c, arrived):
        for w in range(SENT):
            for at in range(SPLIT):
                both_ref[way, c, w, at] = jnp.where(
                    mine[w], both_ref[way, c, w, at], arrived[c, w, at]
                )

    for copy in first_loads:
        copy.wait()
    prepare(0, lambda slot, rows: (slot, rows), key_first, value_first)
    own_taps.wait()
    others = has_left.astype(jnp.int32) + has_right.astype(jnp.int32)
    pl.semaphore_wait(barrier, others + (1 if halves == 2 else 0))
    for step, there in ((-1, has_left), (1, has_right)):
        @pl.when(there)
        def _():
            tap_hop(me, step).start()

    for copy in loads:
        copy.wait()

    drain = HOP * (size - 1) + LEAD
    right_lag = jnp.where(has_right, HOP * me, drain)
    left_lag = jnp.where(has_left, HOP * (size - 1 - me), drain)

    def spread(quad, g_ref):
        start = (quad * QUAD + half * part_rows) % padded_ref.shape[0]
        for g in range(QUAD):
            row = jnp.broadcast_to(padded_ref[pl.ds(start + g, 1), :], (PIECE, width))
            turned = pltpu.roll(row, width - 15, 1, stride=1, stride_axis=0).astype(BF16)
            for n in range(stretches + 2):
                g_ref[g, n] = turned[:, 128 * n : 128 * (n + 1)]

    def compute(quad, which):
        g_ref, next_ref = ((g_even_ref, g_odd_ref), (g_odd_ref, g_even_ref))[which]
        spread(jnp.minimum(quad + 1, 2 * octets - 1), next_ref)
        blocks = []
        for w in range(WIN):
            pieces = []
            for p in range(QUAD):
                c, at = quad * per_quad + p // SPLIT, p % SPLIT
                pieces.append(both_ref[way[w], c, w, at] if w < SENT else own_ref[c, at])
            blocks.append(shifted(pieces))
        zero = jnp.zeros_like(blocks[0][0])

        def column(turn):
            return jnp.concatenate(
                [
                    blocks[w][turn + n - 3] if 0 <= turn + n - 3 < 3 * QUAD else zero
                    for w in range(WIN)
                    for n in range(2 * OCT)
                ],
                axis=0,
            )

        taps = jnp.concatenate(
            [
                jnp.concatenate(
                    [g_ref[g, first[t][w] + h] for w in range(WIN) for h in range(2)], axis=1
                )
                for g in range(QUAD)
                for t in range(slots)
            ],
            axis=0,
        )
        group = lax.broadcasted_iota(jnp.int32, (slots * PIECE, 128), 1) // PIECE % QUAD
        for pair in range(2):
            columns = jnp.concatenate([column(2 * pair), column(2 * pair + 1)], axis=1)
            conv = jnp.dot(taps, columns, preferred_element_type=F32)
            for turn in range(2):
                lanes = slice(128 * turn, 128 * (turn + 1))
                rows = [
                    conv[slots * PIECE * g : slots * PIECE * (g + 1), lanes] for g in range(QUAD)
                ]
                conv_ref[which, 2 * pair + turn] = jnp.where(
                    group < 2,
                    jnp.where(group < 1, rows[0], rows[1]),
                    jnp.where(group < 3, rows[2], rows[3]),
                ).astype(CONV)

    def finish(o):
        lanes = lanes_of(place(o))
        for t in range(slots):
            for turn in range(QUAD):
                rows = slice(PIECE * t, PIECE * (t + 1))
                for half, part in enumerate(
                    swap_halves(conv_ref[0, turn, rows, :], conv_ref[1, turn, rows, :])
                ):
                    start = STRETCH * t + STRETCH // 2 * half + PIECE * turn
                    at = (slice(start, start + PIECE), lanes)
                    out_ref[at] = (query_ref[at].astype(F32) * part.astype(F32)).astype(BF16)

    @pl.loop(0, chunks + drain)
    def _(s):
        far = jnp.where(s == drain, size - 1, jnp.minimum(s // HOP, size - 1))
        turn = (s == drain) | ((s % HOP == jnp.where(far > 1, 1, 0)) & (s // HOP < size - 1))
        for step, onward in ((-1, has_right), (1, has_left)):
            shard = me + step * far
            @pl.when(turn & (far >= 1) & (shard >= 0) & (shard < size))
            def _():
                tap_hop(shard, -step).wait_recv()

                @pl.when(onward)
                def _():
                    tap_hop(shard, -step).start()

                if halves == 2:
                    tap_across(shard, half).start()

        @pl.when((s >= right_lag) & (s < right_lag + chunks))
        def _():
            c = s - right_lag

            @pl.when(has_left)
            def _():
                right_hop(c).wait_recv()
                merge(0, c, from_left_ref)

            @pl.when(has_right)
            def _():
                @pl.when(c >= AHEAD)
                def _():
                    right_hop(c - AHEAD).wait_send()

                right_hop(c).start()

        @pl.when((s >= left_lag) & (s < left_lag + chunks))
        def _():
            c = s - left_lag

            @pl.when(has_right)
            def _():
                left_hop(c).wait_recv()
                merge(1, c, from_right_ref)

            @pl.when(has_left)
            def _():
                @pl.when(c >= AHEAD)
                def _():
                    left_hop(c - AHEAD).wait_send()

                left_hop(c).start()

        @pl.when((s % 2 == 0) & (s // 2 + 1 < octets))
        def _():
            o = s // 2 + 1
            lanes = lanes_of(place(o))
            prepare(o, lambda slot, rows: (slot, rows, lanes), key_ref, value_ref)

        @pl.when(s == drain)
        def _():
            turn_filters(taps_ref, half, padded_ref)
            spread(0, g_even_ref)
            query_load.wait()

        if halves == 2:
            @pl.when(s == drain + chunks // 2 - per_octet)
            def _():
                for shard in range(size):
                    @pl.when(me != shard)
                    def _():
                        tap_across(shard, 1 - half).wait_recv()
                turn_filters(taps_ref, 1 - half, padded_ref)

        for which in range(2):
            @pl.when(
                (s >= drain) & (s < drain + chunks)
                & ((s - drain) % per_octet == per_quad * (which + 1) - 1)
            )
            def _():
                compute((s - drain) // per_quad, which)
                if which == 1:
                    o = (s - drain) // per_octet

                    @pl.when(o >= 2)
                    def _():
                        store(o - 2).wait()

                    finish(o)
                    store(o).start()

        shard = s - drain

        @pl.when((shard >= 0) & (shard <= me) & has_right)
        def _():
            tap_hop(shard, 1).wait_send()

        @pl.when((shard >= me) & (shard < size) & has_left)
        def _():
            tap_hop(shard, -1).wait_send()

        if halves == 2:
            @pl.when((shard >= 0) & (shard < size) & (shard != me))
            def _():
                tap_across(shard, half).wait_send()

    @pl.loop(chunks - AHEAD, chunks)
    def _(c):
        @pl.when(has_right)
        def _():
            right_hop(c).wait_send()

        @pl.when(has_left)
        def _():
            left_hop(c).wait_send()

    store(octets - 2).wait()
    store(octets - 1).wait()


def shards(size, reps, key_proj, value_proj, query_proj, filters, sources, owner):
    rows, channels = key_proj.shape
    groups, span = filters.shape
    stretches = owner.shape[0]
    octets = channels // 128
    slots = rows // STRETCH
    lags = size * span
    chunks = groups // SPLIT
    halves = 2 if reps == 2 else 1
    by_slot = (slots, STRETCH, channels)
    key_proj, value_proj = key_proj.reshape(by_slot), value_proj.reshape(by_slot)
    filters = filters.reshape(halves, groups // halves, span)
    hbm = pl.BlockSpec(memory_space=pltpu.HBM)
    chunk = (chunks, SENT, SPLIT, PIECE, 128)
    dma = pltpu.SemaphoreType.DMA
    return pl.pallas_call(
        functools.partial(fused_kernel, size, halves),
        out_shape=jax.ShapeDtypeStruct((rows, channels), BF16),
        in_specs=[hbm] * 6,
        out_specs=pl.BlockSpec(memory_space=pl.ANY),
        scratch_shapes=[
            pltpu.SMEM(sources.shape, jnp.int32), pltpu.SMEM(owner.shape, jnp.int32),
            pltpu.VMEM((slots, STRETCH, 128), BF16), pltpu.VMEM((slots, STRETCH, 128), BF16),
            pltpu.VMEM(by_slot, BF16), pltpu.VMEM(by_slot, BF16),
            pltpu.VMEM((rows, channels), BF16), pltpu.VMEM((rows, channels), BF16),
            pltpu.VMEM((2,) + chunk, BF16),
            pltpu.VMEM((chunks, SPLIT, PIECE, 128), BF16),
            pltpu.VMEM(chunk, BF16), pltpu.VMEM(chunk, BF16),
            pltpu.VMEM((size, halves, groups // halves, span), BF16),
            pltpu.VMEM((groups, lags + 256), F32),
            pltpu.VMEM((QUAD, stretches + 2, PIECE, 128), BF16),
            pltpu.VMEM((QUAD, stretches + 2, PIECE, 128), BF16),
            pltpu.VMEM((2, QUAD, slots * PIECE, 128), CONV),
            dma((2,)), dma, dma((4,)), dma, dma((2,)),
            dma((size,)), dma((size,)), dma((size,)), dma((size,)), dma((size,)),
            dma((AHEAD,)), dma((chunks,)), dma((AHEAD,)), dma((chunks,)),
        ],
        compiler_params=pltpu.CompilerParams(
            vmem_limit_bytes=55312384, collective_id=0, has_side_effects=True
        ),
    )(sources, owner, key_proj, value_proj, query_proj, filters)


def solution(mesh):
    return jax.shard_map(
        functools.partial(shards, mesh.shape["seq"], mesh.shape["rep"]),
        mesh=mesh,
        in_specs=(
            P(("rep", "seq"), "ch"),
            P(("rep", "seq"), "ch"),
            P(("rep", "seq"), "ch"),
            P("ch", "seq"),
            P("rep"),
            P("rep"),
        ),
        out_specs=P(("rep", "seq"), "ch"),
        check_vma=False,
    )
```

```python
import functools

import jax
import jax.numpy as jnp
from jax import lax
from jax.experimental import pallas as pl
from jax.experimental.pallas import tpu as pltpu
from jax.sharding import PartitionSpec as P

STRETCH = 128
WIN = 4
SENT = WIN - 1
PIECE = 16
OCT = 8
QUAD = 4
SPLIT = 2
HOP = 6
LEAD = 4
SOONER = 4
AHEAD = 8
F32 = jnp.float32
BF16 = jnp.bfloat16
CONV = F32


def swap_halves(low, high):
    keep = lax.broadcasted_iota(jnp.int32, low.shape, 1) < 64
    return (
        jnp.where(keep, low, pltpu.roll(high, 64, 1)),
        jnp.where(keep, pltpu.roll(low, 64, 1), high),
    )


def shifted(pieces):
    keep = lax.broadcasted_iota(jnp.int32, pieces[0].shape, 1) < 64
    zero = jnp.zeros_like(pieces[0])
    turned = [pltpu.roll(piece, 64, 1) for piece in pieces]
    blocks = [jnp.where(keep, zero, piece) for piece in turned]
    blocks += pieces
    blocks += [jnp.where(keep, piece, zero) for piece in turned]
    return blocks


def turn_filters(shards_ref, half, padded_ref):
    count, halves, groups, span = shards_ref.shape
    width = padded_ref.shape[1]
    lags = count * span
    row = lax.broadcasted_iota(jnp.int32, (128, 128), 0)
    col = lax.broadcasted_iota(jnp.int32, (128, 128), 1)
    flip = (row + col == 127).astype(BF16)
    rows = pl.ds(pl.multiple_of(half * groups, groups), groups) if halves == 2 else slice(None)
    for n in range(lags // 128):
        at = lags - 128 * (n + 1)
        chunk = shards_ref[at // span, half, :, at % span : at % span + 128]
        padded_ref[rows, 128 * n : 128 * (n + 1)] = jnp.dot(chunk, flip, preferred_element_type=F32)
    padded_ref[rows, lags:] = jnp.zeros((groups, width - lags), F32)


def fused_kernel(
    size, halves, sources_hbm, owner_hbm, key_hbm, value_hbm, query_hbm, filters_hbm,
    out_ref, sources_ref, owner_ref, key_first, value_first, key_ref, value_ref, query_ref,
    both_ref, own_ref, from_left_ref, from_right_ref, taps_ref, padded_ref, g_even_ref, g_odd_ref,
    conv_ref,
    scalar_sem, own_sem, load_sem, query_sem,
    tap_right_send, tap_left_send, tap_recv, tap_across_send, tap_across_recv,
    right_send, right_recv, left_send, left_recv,
):
    stretches = owner_ref.shape[0]
    slots = key_ref.shape[0]
    octets = out_ref.shape[1] // 128
    width = padded_ref.shape[1]
    last = stretches - 1
    per_quad = QUAD // SPLIT
    per_octet = 2 * per_quad
    chunks = octets * per_octet
    me = lax.axis_index("seq")
    half = lax.axis_index("rep") if halves == 2 else 0
    part_rows = padded_ref.shape[0] // halves
    has_left = me > 0
    has_right = me < size - 1

    def remote(src, dst, send, recv, device):
        return pltpu.make_async_remote_copy(
            src_ref=src, dst_ref=dst, send_sem=send, recv_sem=recv,
            device_id=device, device_id_type=pl.DeviceIdType.MESH,
        )

    def tap_hop(shard, step):
        send = tap_right_send if step > 0 else tap_left_send
        part = taps_ref.at[shard, half]
        return remote(part, part, send.at[shard], tap_recv.at[shard], {"seq": me + step})

    def tap_across(shard, part):
        block = taps_ref.at[shard, part]
        return remote(
            block, block, tap_across_send.at[shard], tap_across_recv.at[shard], {"rep": 1 - half}
        )

    def right_hop(c):
        return remote(
            both_ref.at[0, c], from_left_ref.at[c], right_send.at[c % AHEAD], right_recv.at[c],
            {"seq": me + 1},
        )

    def left_hop(c):
        return remote(
            both_ref.at[1, c], from_right_ref.at[c], left_send.at[c % AHEAD], left_recv.at[c],
            {"seq": me - 1},
        )

    def lanes_of(o):
        if isinstance(o, int):
            return pl.ds(128 * o, 128)
        return pl.ds(pl.multiple_of(o * 128, 128), 128)

    def place(o):
        return (o + half * (octets // 2)) % octets

    first_lanes = lanes_of(place(0))
    first_loads = [
        pltpu.make_async_copy(src.at[:, :, first_lanes], dst, load_sem.at[i])
        for i, (src, dst) in enumerate(((key_hbm, key_first), (value_hbm, value_first)))
    ]
    loads = [
        pltpu.make_async_copy(src, dst, load_sem.at[2 + i])
        for i, (src, dst) in enumerate(((key_hbm, key_ref), (value_hbm, value_ref)))
    ]

    barrier = pltpu.get_barrier_semaphore()

    for step, there in ((-1, has_left), (1, has_right)):
        @pl.when(there)
        def _():
            pl.semaphore_signal(
                barrier, inc=1, device_id={"seq": me + step}, device_id_type=pl.DeviceIdType.MESH
            )

    if halves == 2:
        pl.semaphore_signal(
            barrier, inc=1, device_id={"rep": 1 - half}, device_id_type=pl.DeviceIdType.MESH
        )

    scalars = [
        pltpu.make_async_copy(src, dst, scalar_sem.at[i])
        for i, (src, dst) in enumerate(((sources_hbm, sources_ref), (owner_hbm, owner_ref)))
    ]
    for scalar in scalars:
        scalar.start()
    own_taps = pltpu.make_async_copy(filters_hbm, taps_ref.at[me], own_sem)
    for copy in first_loads:
        copy.start()
    own_taps.start()
    for copy in loads:
        copy.start()
    query_load = pltpu.make_async_copy(query_hbm, query_ref, query_sem)
    query_load.start()

    for scalar in scalars:
        scalar.wait()
    source = [sources_ref[w] for w in range(WIN)]
    source_owner = [jnp.int32(0)] * WIN
    source_slot = [jnp.int32(0)] * WIN
    slot_stretch = [jnp.int32(0)] * slots
    source_owner = [owner_ref[source[w]] for w in range(WIN)]
    count = jnp.int32(0)
    for k in range(stretches):
        holder = owner_ref[k]
        for w in range(WIN - 1):
            source_slot[w] += jnp.where((holder == source_owner[w]) & (k < source[w]), 1, 0)
        here = holder == me
        for t in range(slots):
            slot_stretch[t] += jnp.where(here & (count == t), k, 0)
        count += jnp.where(here, 1, 0)
    first = [
        [last - jnp.maximum(slot_stretch[t] - source[w], -1) for w in range(WIN)]
        for t in range(slots)
    ]
    way = [jnp.where(source_owner[w] <= me, 0, 1) for w in range(WIN - 1)]

    def splat(value):
        return jnp.full((PIECE, 128), value, jnp.int32)

    mine = [splat(source_owner[w]) == me for w in range(WIN)]

    def prepare(o, at_of, keys, values):
        for w in range(WIN):
            slot = source_slot[w] if w < SENT else slots - 1
            parts = []
            for e in range(OCT):
                at = at_of(slot, pl.ds(PIECE * e, PIECE))
                parts.append((keys[at].astype(F32) * values[at].astype(F32)).astype(BF16))
            for p in range(QUAD):
                for quad, part in enumerate(swap_halves(parts[p], parts[p + QUAD])):
                    c, at = o * per_octet + quad * per_quad + p // SPLIT, p % SPLIT
                    if w < SENT:
                        both_ref[0, c, w, at] = part
                        both_ref[1, c, w, at] = part
                    else:
                        own_ref[c, at] = jnp.where(mine[w], part, jnp.zeros_like(part))

    def merge(way, c, arrived):
        for w in range(SENT):
            for at in range(SPLIT):
                both_ref[way, c, w, at] = jnp.where(
                    mine[w], both_ref[way, c, w, at], arrived[c, w, at]
                )

    for copy in first_loads:
        copy.wait()
    prepare(0, lambda slot, rows: (slot, rows), key_first, value_first)
    own_taps.wait()
    others = has_left.astype(jnp.int32) + has_right.astype(jnp.int32)
    pl.semaphore_wait(barrier, others + (1 if halves == 2 else 0))
    for step, there in ((-1, has_left), (1, has_right)):
        @pl.when(there)
        def _():
            tap_hop(me, step).start()

    for copy in loads:
        copy.wait()

    drain = HOP * (size - 1) + LEAD
    right_lag = jnp.where(has_right, HOP * me, drain)
    left_lag = jnp.where(has_left, HOP * (size - 1 - me), drain)

    def spread(quad, g_ref):
        start = (quad * QUAD + half * part_rows) % padded_ref.shape[0]
        for g in range(QUAD):
            row = jnp.broadcast_to(padded_ref[pl.ds(start + g, 1), :], (PIECE, width))
            turned = pltpu.roll(row, width - 15, 1, stride=1, stride_axis=0).astype(BF16)
            for n in range(stretches + 2):
                g_ref[g, n] = turned[:, 128 * n : 128 * (n + 1)]

    def compute(quad, which):
        g_ref, next_ref = ((g_even_ref, g_odd_ref), (g_odd_ref, g_even_ref))[which]
        spread(jnp.minimum(quad + 1, 2 * octets - 1), next_ref)
        blocks = []
        for w in range(WIN):
            pieces = []
            for p in range(QUAD):
                c, at = quad * per_quad + p // SPLIT, p % SPLIT
                pieces.append(both_ref[way[w], c, w, at] if w < SENT else own_ref[c, at])
            blocks.append(shifted(pieces))
        zero = jnp.zeros_like(blocks[0][0])

        def column(turn):
            return jnp.concatenate(
                [
                    blocks[w][turn + n - 3] if 0 <= turn + n - 3 < 3 * QUAD else zero
                    for w in range(WIN)
                    for n in range(2 * OCT)
                ],
                axis=0,
            )

        taps = jnp.concatenate(
            [
                jnp.concatenate(
                    [g_ref[g, first[t][w] + h] for w in range(WIN) for h in range(2)], axis=1
                )
                for g in range(QUAD)
                for t in range(slots)
            ],
            axis=0,
        )
        group = lax.broadcasted_iota(jnp.int32, (slots * PIECE, 128), 1) // PIECE % QUAD
        for pair in range(2):
            columns = jnp.concatenate([column(2 * pair), column(2 * pair + 1)], axis=1)
            conv = jnp.dot(taps, columns, preferred_element_type=F32)
            for turn in range(2):
                lanes = slice(128 * turn, 128 * (turn + 1))
                rows = [
                    conv[slots * PIECE * g : slots * PIECE * (g + 1), lanes] for g in range(QUAD)
                ]
                conv_ref[which, 2 * pair + turn] = jnp.where(
                    group < 2,
                    jnp.where(group < 1, rows[0], rows[1]),
                    jnp.where(group < 3, rows[2], rows[3]),
                ).astype(CONV)

    def finish(o):
        lanes = lanes_of(place(o))
        for t in range(slots):
            for turn in range(QUAD):
                rows = slice(PIECE * t, PIECE * (t + 1))
                for half, part in enumerate(
                    swap_halves(conv_ref[0, turn, rows, :], conv_ref[1, turn, rows, :])
                ):
                    start = STRETCH * t + STRETCH // 2 * half + PIECE * turn
                    at = (slice(start, start + PIECE), lanes)
                    out_ref[at] = (query_ref[at].astype(F32) * part.astype(F32)).astype(BF16)

    begin = drain - jnp.where(has_left & has_right, SOONER, 0)
    streams = (
        (1, left_lag, has_right, has_left, left_hop, from_right_ref),
        (0, right_lag, has_left, has_right, right_hop, from_left_ref),
    )

    @pl.loop(0, (chunks + drain) // 2)
    def _(i):
        s = 2 * i

        @pl.when(s <= drain)
        def _():
            far = jnp.where(s == drain, size - 1, jnp.minimum(s // HOP, size - 1))
            turn = (s == drain) | ((s % HOP == 0) & (s // HOP < size - 1))
            for step, onward in ((-1, has_right), (1, has_left)):
                shard = me + step * far
                @pl.when(turn & (far >= 1) & (shard >= 0) & (shard < size))
                def _():
                    tap_hop(shard, -step).wait_recv()

                    @pl.when(onward)
                    def _():
                        tap_hop(shard, -step).start()

                    if halves == 2:
                        tap_across(shard, half).start()

        for way, lag, upstream, downstream, hop, arrived in streams:
            c = s - lag
            active = (c >= 0) & (c < chunks)

            @pl.when(active & downstream & (c >= AHEAD))
            def _():
                for k in range(2):
                    hop(c + k - AHEAD).wait_send()

            @pl.when(active & upstream & downstream)
            def _():
                for k in range(2):
                    hop(c + k).wait_recv()
                    merge(way, c + k, arrived)
                    hop(c + k).start()

            @pl.when(active & upstream & jnp.logical_not(downstream))
            def _():
                for k in range(2):
                    hop(c + k).wait_recv()
                    merge(way, c + k, arrived)

            @pl.when(active & jnp.logical_not(upstream) & downstream)
            def _():
                for k in range(2):
                    hop(c + k).start()

        @pl.when(i + 1 < octets)
        def _():
            lanes = lanes_of(place(i + 1))
            prepare(i + 1, lambda slot, rows: (slot, rows, lanes), key_ref, value_ref)

        @pl.when(s == begin)
        def _():
            turn_filters(taps_ref, half, padded_ref)
            spread(0, g_even_ref)
            query_load.wait()

        @pl.when(s == begin + chunks // 2 - per_octet)
        def _():
            if halves == 2:
                for shard in range(size):
                    @pl.when(me != shard)
                    def _():
                        tap_across(shard, 1 - half).wait_recv()
                        tap_across(shard, half).wait_send()
                turn_filters(taps_ref, 1 - half, padded_ref)
            for shard in range(size):
                @pl.when((shard <= me) & has_right)
                def _():
                    tap_hop(shard, 1).wait_send()

                @pl.when((shard >= me) & has_left)
                def _():
                    tap_hop(shard, -1).wait_send()

        quad = i - begin // 2
        working = (quad >= 0) & (quad < 2 * octets)

        @pl.when(working & (quad % 2 == 0))
        def _():
            compute(quad, 0)

        @pl.when(working & (quad % 2 == 1))
        def _():
            o = quad // 2
            compute(quad, 1)

            finish(o)

    @pl.loop(chunks - AHEAD, chunks)
    def _(c):
        @pl.when(has_right)
        def _():
            right_hop(c).wait_send()

        @pl.when(has_left)
        def _():
            left_hop(c).wait_send()


def shards(size, reps, key_proj, value_proj, query_proj, filters, sources, owner):
    rows, channels = key_proj.shape
    groups, span = filters.shape
    stretches = owner.shape[0]
    octets = channels // 128
    slots = rows // STRETCH
    lags = size * span
    chunks = groups // SPLIT
    halves = 2 if reps == 2 else 1
    by_slot = (slots, STRETCH, channels)
    key_proj, value_proj = key_proj.reshape(by_slot), value_proj.reshape(by_slot)
    filters = pltpu.with_memory_space_constraint(filters.reshape(halves, groups // halves, span), pltpu.HBM)
    hbm = pl.BlockSpec(memory_space=pltpu.HBM)
    sources = pltpu.with_memory_space_constraint(sources, pltpu.HBM)
    owner = pltpu.with_memory_space_constraint(owner, pltpu.HBM)
    chunk = (chunks, SENT, SPLIT, PIECE, 128)
    dma = pltpu.SemaphoreType.DMA
    return pl.pallas_call(
        functools.partial(fused_kernel, size, halves),
        out_shape=jax.ShapeDtypeStruct((rows, channels), BF16),
        in_specs=[hbm] * 6,
        out_specs=pl.BlockSpec(memory_space=pltpu.VMEM),
        scratch_shapes=[
            pltpu.SMEM(sources.shape, jnp.int32), pltpu.SMEM(owner.shape, jnp.int32),
            pltpu.VMEM((slots, STRETCH, 128), BF16), pltpu.VMEM((slots, STRETCH, 128), BF16),
            pltpu.VMEM(by_slot, BF16), pltpu.VMEM(by_slot, BF16),
            pltpu.VMEM((rows, channels), BF16),
            pltpu.VMEM((2,) + chunk, BF16),
            pltpu.VMEM((chunks, SPLIT, PIECE, 128), BF16),
            pltpu.VMEM(chunk, BF16), pltpu.VMEM(chunk, BF16),
            pltpu.VMEM((size, halves, groups // halves, span), BF16),
            pltpu.VMEM((groups, lags + 256), F32),
            pltpu.VMEM((QUAD, stretches + 2, PIECE, 128), BF16),
            pltpu.VMEM((QUAD, stretches + 2, PIECE, 128), BF16),
            pltpu.VMEM((2, QUAD, slots * PIECE, 128), CONV),
            dma((2,)), dma, dma((4,)), dma,
            dma((size,)), dma((size,)), dma((size,)), dma((size,)), dma((size,)),
            dma((AHEAD,)), dma((chunks,)), dma((AHEAD,)), dma((chunks,)),
        ],
        compiler_params=pltpu.CompilerParams(
            vmem_limit_bytes=55312384, collective_id=0, has_side_effects=True
        ),
    )(sources, owner, key_proj, value_proj, query_proj, filters)


def solution(mesh):
    return jax.shard_map(
        functools.partial(shards, mesh.shape["seq"], mesh.shape["rep"]),
        mesh=mesh,
        in_specs=(
            P(("rep", "seq"), "ch"),
            P(("rep", "seq"), "ch"),
            P(("rep", "seq"), "ch"),
            P("ch", "seq"),
            P("rep"),
            P("rep"),
        ),
        out_specs=P(("rep", "seq"), "ch"),
        check_vma=False,
    )
```

```python
import functools

import jax
import jax.numpy as jnp
from jax import lax
from jax.experimental import pallas as pl
from jax.experimental.pallas import tpu as pltpu
from jax.sharding import PartitionSpec as P

STRETCH = 128
WIN = 4
SENT = WIN - 1
PIECE = 16
OCT = 8
QUAD = 4
SPLIT = 2
HOP = 6
LEAD = 4
SOONER = 4
FIRST = 2
AHEAD = 8
F32 = jnp.float32
BF16 = jnp.bfloat16
CONV = F32


def swap_halves(low, high):
    keep = lax.broadcasted_iota(jnp.int32, low.shape, 1) < 64
    return (
        jnp.where(keep, low, pltpu.roll(high, 64, 1)),
        jnp.where(keep, pltpu.roll(low, 64, 1), high),
    )


def shifted(pieces):
    keep = lax.broadcasted_iota(jnp.int32, pieces[0].shape, 1) < 64
    zero = jnp.zeros_like(pieces[0])
    turned = [pltpu.roll(piece, 64, 1) for piece in pieces]
    blocks = [jnp.where(keep, zero, piece) for piece in turned]
    blocks += pieces
    blocks += [jnp.where(keep, piece, zero) for piece in turned]
    return blocks


def turn_filters(shards_ref, half, padded_ref):
    count, halves, groups, span = shards_ref.shape
    width = padded_ref.shape[1]
    lags = count * span
    row = lax.broadcasted_iota(jnp.int32, (128, 128), 0)
    col = lax.broadcasted_iota(jnp.int32, (128, 128), 1)
    flip = (row + col == 127).astype(BF16)
    rows = pl.ds(pl.multiple_of(half * groups, groups), groups) if halves == 2 else slice(None)
    for n in range(lags // 128):
        at = lags - 128 * (n + 1)
        chunk = shards_ref[at // span, half, :, at % span : at % span + 128]
        padded_ref[rows, 128 * n : 128 * (n + 1)] = jnp.dot(chunk, flip, preferred_element_type=F32)
    padded_ref[rows, lags:] = jnp.zeros((groups, width - lags), F32)


def fused_kernel(
    size, halves, sources_hbm, owner_hbm, key_hbm, value_hbm, query_hbm, filters_hbm,
    out_ref, sources_ref, owner_ref, key_first, value_first, key_ref, value_ref, query_ref,
    both_ref, own_ref, from_left_ref, from_right_ref, taps_ref, padded_ref, g_even_ref, g_odd_ref,
    conv_ref,
    scalar_sem, own_sem, load_sem, query_sem,
    tap_right_send, tap_left_send, tap_recv, tap_across_send, tap_across_recv,
    right_send, right_recv, left_send, left_recv,
):
    stretches = owner_ref.shape[0]
    slots = key_ref.shape[0]
    octets = out_ref.shape[1] // 128
    width = padded_ref.shape[1]
    last = stretches - 1
    per_quad = QUAD // SPLIT
    per_octet = 2 * per_quad
    chunks = octets * per_octet
    me = lax.axis_index("seq")
    half = lax.axis_index("rep") if halves == 2 else 0
    part_rows = padded_ref.shape[0] // halves
    has_left = me > 0
    has_right = me < size - 1

    def remote(src, dst, send, recv, device):
        return pltpu.make_async_remote_copy(
            src_ref=src, dst_ref=dst, send_sem=send, recv_sem=recv,
            device_id=device, device_id_type=pl.DeviceIdType.MESH,
        )

    def tap_hop(shard, step):
        send = tap_right_send if step > 0 else tap_left_send
        part = taps_ref.at[shard, half]
        return remote(part, part, send.at[shard], tap_recv.at[shard], {"seq": me + step})

    def tap_across(shard, part):
        block = taps_ref.at[shard, part]
        return remote(
            block, block, tap_across_send.at[shard], tap_across_recv.at[shard], {"rep": 1 - half}
        )

    def right_hop(c):
        return remote(
            both_ref.at[0, c], from_left_ref.at[c], right_send.at[c % AHEAD], right_recv.at[c],
            {"seq": me + 1},
        )

    def left_hop(c):
        return remote(
            both_ref.at[1, c], from_right_ref.at[c], left_send.at[c % AHEAD], left_recv.at[c],
            {"seq": me - 1},
        )

    def lanes_of(o):
        if isinstance(o, int):
            return pl.ds(128 * o, 128)
        return pl.ds(pl.multiple_of(o * 128, 128), 128)

    def place(o):
        return (o + half * (octets // 2)) % octets

    first_lanes = lanes_of(place(0))
    first_loads = [
        pltpu.make_async_copy(src.at[:, :, first_lanes], dst, load_sem.at[i])
        for i, (src, dst) in enumerate(((key_hbm, key_first), (value_hbm, value_first)))
    ]
    loads = [
        pltpu.make_async_copy(src, dst, load_sem.at[2 + i])
        for i, (src, dst) in enumerate(((key_hbm, key_ref), (value_hbm, value_ref)))
    ]

    barrier = pltpu.get_barrier_semaphore()

    for step, there in ((-1, has_left), (1, has_right)):
        @pl.when(there)
        def _():
            pl.semaphore_signal(
                barrier, inc=1, device_id={"seq": me + step}, device_id_type=pl.DeviceIdType.MESH
            )

    if halves == 2:
        pl.semaphore_signal(
            barrier, inc=1, device_id={"rep": 1 - half}, device_id_type=pl.DeviceIdType.MESH
        )

    scalars = [
        pltpu.make_async_copy(src, dst, scalar_sem.at[i])
        for i, (src, dst) in enumerate(((sources_hbm, sources_ref), (owner_hbm, owner_ref)))
    ]
    for scalar in scalars:
        scalar.start()
    own_taps = pltpu.make_async_copy(filters_hbm, taps_ref.at[me], own_sem)
    for copy in first_loads:
        copy.start()
    own_taps.start()
    for copy in loads:
        copy.start()
    query_load = pltpu.make_async_copy(query_hbm, query_ref, query_sem)
    query_load.start()

    for scalar in scalars:
        scalar.wait()
    source = [sources_ref[w] for w in range(WIN)]
    source_owner = [jnp.int32(0)] * WIN
    source_slot = [jnp.int32(0)] * WIN
    slot_stretch = [jnp.int32(0)] * slots
    source_owner = [owner_ref[source[w]] for w in range(WIN)]
    count = jnp.int32(0)
    for k in range(stretches):
        holder = owner_ref[k]
        for w in range(WIN - 1):
            source_slot[w] += jnp.where((holder == source_owner[w]) & (k < source[w]), 1, 0)
        here = holder == me
        for t in range(slots):
            slot_stretch[t] += jnp.where(here & (count == t), k, 0)
        count += jnp.where(here, 1, 0)
    first = [
        [last - jnp.maximum(slot_stretch[t] - source[w], -1) for w in range(WIN)]
        for t in range(slots)
    ]
    way = [jnp.where(source_owner[w] <= me, 0, 1) for w in range(WIN - 1)]

    def splat(value):
        return jnp.full((PIECE, 128), value, jnp.int32)

    mine = [splat(source_owner[w]) == me for w in range(WIN)]

    def prepare(o, at_of, keys, values):
        for w in range(WIN):
            slot = source_slot[w] if w < SENT else slots - 1
            parts = []
            for e in range(OCT):
                at = at_of(slot, pl.ds(PIECE * e, PIECE))
                parts.append((keys[at].astype(F32) * values[at].astype(F32)).astype(BF16))
            for p in range(QUAD):
                for quad, part in enumerate(swap_halves(parts[p], parts[p + QUAD])):
                    c, at = o * per_octet + quad * per_quad + p // SPLIT, p % SPLIT
                    if w < SENT:
                        both_ref[0, c, w, at] = part
                        both_ref[1, c, w, at] = part
                    else:
                        own_ref[c, at] = jnp.where(mine[w], part, jnp.zeros_like(part))

    def merge(way, c, arrived):
        for w in range(SENT):
            for at in range(SPLIT):
                both_ref[way, c, w, at] = jnp.where(
                    mine[w], both_ref[way, c, w, at], arrived[c, w, at]
                )

    for copy in first_loads:
        copy.wait()
    prepare(0, lambda slot, rows: (slot, rows), key_first, value_first)
    own_taps.wait()
    others = has_left.astype(jnp.int32) + has_right.astype(jnp.int32)
    pl.semaphore_wait(barrier, others + (1 if halves == 2 else 0))
    for upstream, downstream, hop in (
        (has_right, has_left, left_hop), (has_left, has_right, right_hop),
    ):
        @pl.when(jnp.logical_not(upstream) & downstream)
        def _():
            for c in range(FIRST):
                hop(c).start()

    for step, there in ((-1, has_left), (1, has_right)):
        @pl.when(there)
        def _():
            tap_hop(me, step).start()

    for copy in loads:
        copy.wait()

    drain = HOP * (size - 1) + LEAD
    right_lag = jnp.where(has_right, HOP * me, drain)
    left_lag = jnp.where(has_left, HOP * (size - 1 - me), drain)

    def spread(quad, g_ref):
        start = (quad * QUAD + half * part_rows) % padded_ref.shape[0]
        for g in range(QUAD):
            row = jnp.broadcast_to(padded_ref[pl.ds(start + g, 1), :], (PIECE, width))
            turned = pltpu.roll(row, width - 15, 1, stride=1, stride_axis=0).astype(BF16)
            for n in range(stretches + 2):
                g_ref[g, n] = turned[:, 128 * n : 128 * (n + 1)]

    def compute(quad, which):
        g_ref, next_ref = ((g_even_ref, g_odd_ref), (g_odd_ref, g_even_ref))[which]
        spread(jnp.minimum(quad + 1, 2 * octets - 1), next_ref)
        blocks = []
        for w in range(WIN):
            pieces = []
            for p in range(QUAD):
                c, at = quad * per_quad + p // SPLIT, p % SPLIT
                pieces.append(both_ref[way[w], c, w, at] if w < SENT else own_ref[c, at])
            blocks.append(shifted(pieces))
        zero = jnp.zeros_like(blocks[0][0])

        def column(turn):
            return jnp.concatenate(
                [
                    blocks[w][turn + n - 3] if 0 <= turn + n - 3 < 3 * QUAD else zero
                    for w in range(WIN)
                    for n in range(2 * OCT)
                ],
                axis=0,
            )

        taps = jnp.concatenate(
            [
                jnp.concatenate(
                    [g_ref[g, first[t][w] + h] for w in range(WIN) for h in range(2)], axis=1
                )
                for g in range(QUAD)
                for t in range(slots)
            ],
            axis=0,
        )
        group = lax.broadcasted_iota(jnp.int32, (slots * PIECE, 128), 1) // PIECE % QUAD
        for pair in range(2):
            columns = jnp.concatenate([column(2 * pair), column(2 * pair + 1)], axis=1)
            conv = jnp.dot(taps, columns, preferred_element_type=F32)
            for turn in range(2):
                lanes = slice(128 * turn, 128 * (turn + 1))
                rows = [
                    conv[slots * PIECE * g : slots * PIECE * (g + 1), lanes] for g in range(QUAD)
                ]
                conv_ref[which, 2 * pair + turn] = jnp.where(
                    group < 2,
                    jnp.where(group < 1, rows[0], rows[1]),
                    jnp.where(group < 3, rows[2], rows[3]),
                ).astype(CONV)

    def finish(o):
        lanes = lanes_of(place(o))
        for t in range(slots):
            for turn in range(QUAD):
                rows = slice(PIECE * t, PIECE * (t + 1))
                for half, part in enumerate(
                    swap_halves(conv_ref[0, turn, rows, :], conv_ref[1, turn, rows, :])
                ):
                    start = STRETCH * t + STRETCH // 2 * half + PIECE * turn
                    at = (slice(start, start + PIECE), lanes)
                    out_ref[at] = (query_ref[at].astype(F32) * part.astype(F32)).astype(BF16)

    begin = drain - jnp.where(has_left & has_right, SOONER, 0)
    streams = (
        (1, left_lag, has_right, has_left, left_hop, from_right_ref),
        (0, right_lag, has_left, has_right, right_hop, from_left_ref),
    )

    @pl.loop(0, (chunks + drain) // 2)
    def _(i):
        s = 2 * i

        for way, lag, upstream, downstream, hop, arrived in streams:
            c = s - lag
            active = (c >= 0) & (c < chunks)

            @pl.when(active & downstream & (c >= AHEAD))
            def _():
                for k in range(2):
                    hop(c + k - AHEAD).wait_send()

            @pl.when(active & upstream & downstream)
            def _():
                for k in range(2):
                    hop(c + k).wait_recv()
                    merge(way, c + k, arrived)
                    hop(c + k).start()

            @pl.when(active & upstream & jnp.logical_not(downstream))
            def _():
                for k in range(2):
                    hop(c + k).wait_recv()
                    merge(way, c + k, arrived)

            @pl.when(active & jnp.logical_not(upstream) & downstream & (c >= FIRST))
            def _():
                for k in range(2):
                    hop(c + k).start()

        @pl.when(s <= drain)
        def _():
            far = jnp.where(s == drain, size - 1, jnp.minimum(s // HOP, size - 1))
            turn = (s == drain) | ((s % HOP == 0) & (s // HOP < size - 1))
            for step, onward in ((-1, has_right), (1, has_left)):
                shard = me + step * far
                @pl.when(turn & (far >= 1) & (shard >= 0) & (shard < size))
                def _():
                    tap_hop(shard, -step).wait_recv()

                    @pl.when(onward)
                    def _():
                        tap_hop(shard, -step).start()

                    if halves == 2:
                        tap_across(shard, half).start()

        @pl.when(i + 1 < octets)
        def _():
            lanes = lanes_of(place(i + 1))
            prepare(i + 1, lambda slot, rows: (slot, rows, lanes), key_ref, value_ref)

        @pl.when(s == begin)
        def _():
            turn_filters(taps_ref, half, padded_ref)
            spread(0, g_even_ref)
            query_load.wait()

        @pl.when(s == begin + chunks // 2 - per_octet)
        def _():
            if halves == 2:
                for shard in range(size):
                    @pl.when(me != shard)
                    def _():
                        tap_across(shard, 1 - half).wait_recv()
                        tap_across(shard, half).wait_send()
                turn_filters(taps_ref, 1 - half, padded_ref)
            for shard in range(size):
                @pl.when((shard <= me) & has_right)
                def _():
                    tap_hop(shard, 1).wait_send()

                @pl.when((shard >= me) & has_left)
                def _():
                    tap_hop(shard, -1).wait_send()

        quad = i - begin // 2
        working = (quad >= 0) & (quad < 2 * octets)

        @pl.when(working & (quad % 2 == 0))
        def _():
            compute(quad, 0)

        @pl.when(working & (quad % 2 == 1))
        def _():
            o = quad // 2
            compute(quad, 1)

            finish(o)

    @pl.loop(chunks - AHEAD, chunks)
    def _(c):
        @pl.when(has_right)
        def _():
            right_hop(c).wait_send()

        @pl.when(has_left)
        def _():
            left_hop(c).wait_send()


def shards(size, reps, key_proj, value_proj, query_proj, filters, sources, owner):
    rows, channels = key_proj.shape
    groups, span = filters.shape
    stretches = owner.shape[0]
    octets = channels // 128
    slots = rows // STRETCH
    lags = size * span
    chunks = groups // SPLIT
    halves = 2 if reps == 2 else 1
    by_slot = (slots, STRETCH, channels)
    key_proj, value_proj = key_proj.reshape(by_slot), value_proj.reshape(by_slot)
    filters = pltpu.with_memory_space_constraint(filters.reshape(halves, groups // halves, span), pltpu.HBM)
    hbm = pl.BlockSpec(memory_space=pltpu.HBM)
    sources = pltpu.with_memory_space_constraint(sources, pltpu.HBM)
    owner = pltpu.with_memory_space_constraint(owner, pltpu.HBM)
    chunk = (chunks, SENT, SPLIT, PIECE, 128)
    dma = pltpu.SemaphoreType.DMA
    return pl.pallas_call(
        functools.partial(fused_kernel, size, halves),
        out_shape=jax.ShapeDtypeStruct((rows, channels), BF16),
        in_specs=[hbm] * 6,
        out_specs=pl.BlockSpec(memory_space=pltpu.VMEM),
        scratch_shapes=[
            pltpu.SMEM(sources.shape, jnp.int32), pltpu.SMEM(owner.shape, jnp.int32),
            pltpu.VMEM((slots, STRETCH, 128), BF16), pltpu.VMEM((slots, STRETCH, 128), BF16),
            pltpu.VMEM(by_slot, BF16), pltpu.VMEM(by_slot, BF16),
            pltpu.VMEM((rows, channels), BF16),
            pltpu.VMEM((2,) + chunk, BF16),
            pltpu.VMEM((chunks, SPLIT, PIECE, 128), BF16),
            pltpu.VMEM(chunk, BF16), pltpu.VMEM(chunk, BF16),
            pltpu.VMEM((size, halves, groups // halves, span), BF16),
            pltpu.VMEM((groups, lags + 256), F32),
            pltpu.VMEM((QUAD, stretches + 2, PIECE, 128), BF16),
            pltpu.VMEM((QUAD, stretches + 2, PIECE, 128), BF16),
            pltpu.VMEM((2, QUAD, slots * PIECE, 128), CONV),
            dma((2,)), dma, dma((4,)), dma,
            dma((size,)), dma((size,)), dma((size,)), dma((size,)), dma((size,)),
            dma((AHEAD,)), dma((chunks,)), dma((AHEAD,)), dma((chunks,)),
        ],
        compiler_params=pltpu.CompilerParams(
            vmem_limit_bytes=55312384, collective_id=0, has_side_effects=True
        ),
    )(sources, owner, key_proj, value_proj, query_proj, filters)


def solution(mesh):
    return jax.shard_map(
        functools.partial(shards, mesh.shape["seq"], mesh.shape["rep"]),
        mesh=mesh,
        in_specs=(
            P(("rep", "seq"), "ch"),
            P(("rep", "seq"), "ch"),
            P(("rep", "seq"), "ch"),
            P("ch", "seq"),
            P("rep"),
            P("rep"),
        ),
        out_specs=P(("rep", "seq"), "ch"),
        check_vma=False,
    )
```
